128 devices in a mesh: batch: 2 (over x_hi), blk: 64 (over x_lo, z, y, core).
Axes of the slice: x: 4 (x_hi: 2, x_lo: 2; x = x_hi * 2 + x_lo), y: 4, z: 4, core: 2. Of those that a mesh axis runs over, the one named last changes fastest.
Arguments:
- stream: bfloat16 [131072, 1024], P(('batch', 'blk')), parts along dimension 0, may hold values from -6 to 6
- norm_gain: float32 [4, 1024], replicated, may hold values from 0.1 to 1.9
- norm_bias: float32 [4, 1024], replicated, may hold values from -3 to 3
- proj_in: bfloat16 [4, 1024, 512], replicated, may hold values from -0.1875 to 0.1875
- convolution_taps: bfloat16 [4, 3, 512, 512], replicated, may hold values from -0.15625 to 0.15625
- output_projection: bfloat16 [4, 512, 1024], replicated, may hold values from -0.25 to 0.25
Outputs:
- result: bfloat16 [131072, 1024], P(('batch', 'blk')), parts along dimension 0
The draws below stay inside these ranges and needn't reach their ends.
There are 2 independent parts, one for each index of `batch`. The reference program is written for one: setup_inputs(seed, part) draws one part's arguments, and reference() takes and returns one part's arrays. A program takes and returns all parts, laid end to end along the dimension named above; an argument that names none is the same for every part. Nothing has to cross between parts.
All inputs are finite; a program needn't handle non-finite values.
Results may differ from the reference program's by a relative error of at most 0.017.
Values may be sent and summed in bfloat16 or wider, within the bound.
A program may use at most 64 MiB of HBM per device.

```python
import jax
import jax.numpy as jnp
from jax import lax

D = 1024
H = 512
LAYERS = 4
DILATION_START = 512
SEQ = 65536


def block_levels(rng, dims, pieces, least, high):
    def one(position, parts):
        steps = jax.random.uniform(jax.random.fold_in(jax.random.fold_in(rng, 6), position), (parts,), jnp.float32, least / len(pieces), high / len(pieces))
        return jnp.repeat(jnp.exp(steps), dims[position] // parts).reshape((-1,) + (1,) * (len(dims) - position - 1))

    factor_of = one(*pieces[0])
    for cut in pieces[1:]:
        factor_of = factor_of * one(*cut)
    return factor_of


def scatter_about(stream_key, dims, deviation, limit, split=(), dtype=jnp.bfloat16):
    array = jax.random.normal(stream_key, dims, jnp.float32) * deviation
    if len(split) > 0:
        array = block_levels(stream_key, dims, split, -0.22, 0.18) * array
    return jnp.clip(array, min=-limit, max=limit).astype(dtype)


def setup_inputs(seed: int = 0, part: int = 0) -> dict:
    keys = jax.random.split(jax.random.key(seed), 7)
    part_splits = jax.random.split(jax.random.fold_in(keys[6], part), 7)
    stream = scatter_about(part_splits[0], (SEQ, D), 1.0, 6.0, ((0, 64),))
    norm_gain = jnp.clip(1.0 + 0.18 * jax.random.normal(keys[1], (LAYERS, D), jnp.float32), 0.1, 1.9)
    norm_bias = scatter_about(keys[2], (LAYERS, D), 0.5, 3.0, (), jnp.float32)
    proj_in = scatter_about(keys[3], (LAYERS, D, H), D ** -0.5, 0.1875)
    convolution_taps = scatter_about(keys[4], (LAYERS, 3, H, H), (3 * H) ** -0.5, 0.15625)
    output_projection = scatter_about(keys[5], (LAYERS, H, D), H ** -0.5, 0.25)
    return {"stream": stream, "norm_gain": norm_gain, "norm_bias": norm_bias, "proj_in": proj_in, "convolution_taps": convolution_taps, "output_projection": output_projection}


EPSILON = 1e-05

def normalize(stream, scales, offsets):
    values = stream.astype(jnp.float32)
    average = lax.optimization_barrier(jnp.mean(values, axis=1, keepdims=True))
    centred_values = values - average
    variance = lax.optimization_barrier(jnp.mean(centred_values * centred_values, axis=1, keepdims=True))
    return (centred_values * jax.lax.rsqrt(variance + EPSILON) * scales + offsets).astype(jnp.bfloat16)

def reference(stream, norm_gain, norm_bias, proj_in, convolution_taps, output_projection):
    for block_depth in range(LAYERS):
        dilation_factor = DILATION_START * 2 ** block_depth
        normed = normalize(stream, norm_gain[block_depth], norm_bias[block_depth])
        narrow = jnp.dot(normed, proj_in[block_depth], preferred_element_type=jnp.float32).astype(jnp.bfloat16)
        kernel = convolution_taps[block_depth]
        convolved = jnp.dot(jnp.roll(narrow, dilation_factor, axis=0), kernel[0], preferred_element_type=jnp.float32)
        convolved = convolved + jnp.dot(narrow, kernel[1], preferred_element_type=jnp.float32)
        convolved = convolved + jnp.dot(jnp.roll(narrow, -dilation_factor, axis=0), kernel[2], preferred_element_type=jnp.float32)
        activated = jax.nn.gelu(convolved, approximate=False).astype(jnp.bfloat16)
        update = jnp.dot(activated, output_projection[block_depth], preferred_element_type=jnp.float32)
        stream = (stream.astype(jnp.float32) + update).astype(jnp.bfloat16)
    return stream
```

```python
import functools

import jax
import jax.numpy as jnp
from jax import lax
from jax.experimental import pallas as pl
from jax.experimental.pallas import tpu as pltpu
from jax.sharding import PartitionSpec as P

MESH = pl.DeviceIdType.MESH
LAYERS = 4
UNIT = 512
EPSILON = 1e-05
GROUP = 8
SLAB = 16
BF16 = jnp.bfloat16
F32 = jnp.float32


def gelu(values):
    return 0.5 * values * (1.0 + lax.erf(values * 0.7071067811865476))


def kernel(
    peers, halves, chunks,
    x_hbm, gain_ref, bias_ref, proj_hbm, taps_hbm, outp_hbm,
    out_hbm,
    xt, narrow, proj, taps, outp,
    in_send, in_recv, own_sem, halo_send, halo_recv, out_send, out_recv, out_own, weight_sem,
):
    me = lax.axis_index("blk")
    rank = lax.rem(me, GROUP)
    base = me - rank
    above = lax.rem(me + GROUP, peers)
    below = lax.rem(me + peers - GROUP, peers)
    span = GROUP * halves
    rows = span * SLAB
    width = x_hbm.shape[-1]
    hidden = narrow.shape[-1]

    def mate(step):
        return lax.rem(rank + step, GROUP)

    def remote(src, dst, send, recv, device):
        return pltpu.make_async_remote_copy(
            src_ref=src, dst_ref=dst, send_sem=send, recv_sem=recv,
            device_id={"blk": device}, device_id_type=MESH,
        )

    def weight_copies(layer):
        return (
            pltpu.make_async_copy(proj_hbm.at[layer], proj.at[layer], weight_sem.at[layer, 0]),
            pltpu.make_async_copy(taps_hbm.at[layer], taps.at[layer], weight_sem.at[layer, 1]),
            pltpu.make_async_copy(outp_hbm.at[layer], outp.at[layer], weight_sem.at[layer, 2]),
        )

    def own_in(chunk):
        return pltpu.make_async_copy(
            x_hbm.at[:, rank, chunk], xt.at[chunk, pl.ds(halves * rank, halves)], own_sem.at[chunk]
        )

    for copy in weight_copies(0):
        copy.start()

    @pl.loop(0, chunks)
    def _(chunk):
        own_in(chunk).start()

    barrier = pltpu.get_barrier_semaphore()
    for step in range(1, GROUP):
        pl.semaphore_signal(barrier, inc=1, device_id={"blk": base + mate(step)}, device_id_type=MESH)
    for device in (above, below):
        pl.semaphore_signal(barrier, inc=1, device_id={"blk": device}, device_id_type=MESH)
    pl.semaphore_wait(barrier, GROUP + 1)

    @pl.loop(0, chunks)
    def _(chunk):
        for step in (4, 5, 3, 6, 2, 7, 1):
            to = mate(step)
            remote(
                x_hbm.at[:, to, chunk], xt.at[chunk, pl.ds(halves * rank, halves)],
                in_send.at[chunk], in_recv.at[chunk], base + to,
            ).start()

    for layer in range(1, LAYERS):
        for copy in weight_copies(layer):
            copy.start()

    def halo_copies(layer, chunk):
        reach = 2**layer
        mine = narrow.at[chunk, layer]
        up = remote(
            mine.at[pl.ds(span // 2 + span - reach, reach)], mine.at[pl.ds(span // 2 - reach, reach)],
            halo_send.at[chunk, layer, 0], halo_recv.at[chunk, layer, 0], above,
        )
        down = remote(
            mine.at[pl.ds(span // 2, reach)], mine.at[pl.ds(span // 2 + span, reach)],
            halo_send.at[chunk, layer, 1], halo_recv.at[chunk, layer, 1], below,
        )
        return up, down

    def project(layer, chunk):
        values = xt[chunk].reshape(rows, width).astype(F32)
        centred = values - jnp.mean(values, axis=1, keepdims=True)
        variance = jnp.mean(centred * centred, axis=1, keepdims=True)
        normed = centred * lax.rsqrt(variance + EPSILON) * gain_ref[pl.ds(layer, 1), :] + bias_ref[pl.ds(layer, 1), :]
        result = jnp.dot(normed.astype(BF16), proj[layer], preferred_element_type=F32).astype(BF16)
        narrow[chunk, layer, pl.ds(span // 2, span)] = result.reshape(span, SLAB, hidden)

    def update(layer, reach, chunk):
        parts = [
            narrow[chunk, layer, pl.ds(span // 2 + shift, span)].reshape(rows, hidden)
            for shift in (-reach, 0, reach)
        ]
        convolved = jnp.dot(
            jnp.concatenate(parts, axis=1), taps[layer], preferred_element_type=F32
        )
        activated = gelu(convolved).astype(BF16)
        delta = jnp.dot(activated, outp[layer], preferred_element_type=F32)
        new = (xt[chunk].reshape(rows, width).astype(F32) + delta).astype(BF16)
        xt[chunk] = new.reshape(span, SLAB, width)

    def own_out(chunk):
        return pltpu.make_async_copy(
            xt.at[chunk, pl.ds(halves * rank, halves)], out_hbm.at[:, rank, chunk], out_own.at[chunk]
        )

    def out_copies(chunk):
        return [
            remote(
                xt.at[chunk, pl.ds(halves * mate(step), halves)], out_hbm.at[:, rank, chunk],
                out_send.at[chunk], out_recv.at[chunk], base + mate(step),
            )
            for step in (4, 5, 3, 6, 2, 7, 1)
        ]

    stages = LAYERS + 1

    @pl.loop(0, stages + chunks - 1)
    def _(wave):
        @pl.loop(0, chunks)
        def _(chunk):
            stage = wave - chunk

            @pl.when(stage == 0)
            def _():
                own_in(chunk).wait()
                whole = xt.at[chunk, pl.ds(0, span - halves)]
                pltpu.make_async_copy(whole, whole, in_recv.at[chunk]).wait()

            for layer in range(LAYERS):
                @pl.when((stage == layer) & (chunk == 0))
                def _():
                    for copy in weight_copies(layer):
                        copy.wait()

                @pl.when(stage == layer + 1)
                def _():
                    for copy in halo_copies(layer, chunk):
                        copy.wait_recv()
                    update(layer, 2**layer, chunk)

                @pl.when(stage == layer)
                def _():
                    project(layer, chunk)
                    for copy in halo_copies(layer, chunk):
                        copy.start()

            @pl.when(stage == LAYERS)
            def _():
                own_out(chunk).start()
                for copy in out_copies(chunk):
                    copy.start()

    @pl.loop(0, chunks)
    def _(chunk):
        whole = xt.at[chunk, pl.ds(0, span - halves)]
        own_out(chunk).wait()
        for layer in range(LAYERS):
            for copy in halo_copies(layer, chunk):
                copy.wait_send()
        pltpu.make_async_copy(whole, whole, in_send.at[chunk]).wait()
        pltpu.make_async_copy(whole, whole, out_send.at[chunk]).wait()
        pltpu.make_async_copy(whole, whole, out_recv.at[chunk]).wait()


def solution(mesh):
    peers = mesh.shape["blk"]

    def body(stream, norm_gain, norm_bias, proj_in, convolution_taps, output_projection):
        rows, width = stream.shape
        hidden = proj_in.shape[2]
        halves = rows // UNIT
        chunks = UNIT // GROUP // SLAB
        span = GROUP * halves
        shape = (halves, GROUP, chunks, SLAB, width)
        vmem = pl.BlockSpec(memory_space=pltpu.VMEM)
        anywhere = pl.BlockSpec(memory_space=pl.ANY)
        dma = pltpu.SemaphoreType.DMA
        result = pl.pallas_call(
            functools.partial(kernel, peers, halves, chunks),
            out_shape=jax.ShapeDtypeStruct(shape, BF16),
            in_specs=[anywhere, vmem, vmem, anywhere, anywhere, anywhere],
            out_specs=anywhere,
            scratch_shapes=[
                pltpu.VMEM((chunks, span, SLAB, width), BF16),
                pltpu.VMEM((chunks, LAYERS, 2 * span, SLAB, hidden), BF16),
                pltpu.VMEM((LAYERS, width, hidden), BF16),
                pltpu.VMEM((LAYERS, 3 * hidden, hidden), BF16),
                pltpu.VMEM((LAYERS, hidden, width), BF16),
                dma((chunks,)), dma((chunks,)), dma((chunks,)),
                dma((chunks, LAYERS, 2)), dma((chunks, LAYERS, 2)),
                dma((chunks,)), dma((chunks,)), dma((chunks,)),
                dma((LAYERS, 3)),
            ],
            compiler_params=pltpu.CompilerParams(
                collective_id=0, has_side_effects=True, vmem_limit_bytes=56 * 2**20
            ),
        )(
            stream.reshape(shape), norm_gain, norm_bias, proj_in,
            convolution_taps.reshape(LAYERS, 3 * hidden, hidden), output_projection,
        )
        return result.reshape(rows, width)

    return jax.shard_map(
        body,
        mesh=mesh,
        in_specs=(P(("batch", "blk"), None), P(), P(), P(), P(), P()),
        out_specs=P(("batch", "blk"), None),
        check_vma=False,
    )
```

```python
import functools

import jax
import jax.numpy as jnp
from jax import lax
from jax.experimental import pallas as pl
from jax.experimental.pallas import tpu as pltpu
from jax.sharding import PartitionSpec as P

MESH = pl.DeviceIdType.MESH
LAYERS = 4
UNIT = 512
EPSILON = 1e-05
GROUP = 8
SLAB = 16
ORDER = ((2, 0), (2, 1), (1, 0), (3, 0), (1, 1), (3, 1), (0, 1))
AHEAD = 4
SCHEDULE = (0, 10, 1, 20, 11, 2, 30, 21, 12, 3, 40, 31, 22, 13, 41, 32, 23, 42, 33, 43)
BF16 = jnp.bfloat16
F32 = jnp.float32


def gelu(values):
    return 0.5 * values * (1.0 + lax.erf(values * 0.7071067811865476))


def kernel(
    peers, halves, chunks,
    x_hbm, gain_ref, bias_ref, proj_hbm, taps_hbm, outp_hbm,
    out_ref,
    xt, narrow, proj, taps, outp,
    in_send, in_recv, own_sem, halo_send, halo_recv, out_send, out_recv, out_own, weight_sem,
):
    me = lax.axis_index("blk")
    rank = lax.rem(me, GROUP)
    base = me - rank
    above = lax.rem(me + GROUP, peers)
    below = lax.rem(me + peers - GROUP, peers)
    span = GROUP * halves
    rows = span * SLAB
    width = x_hbm.shape[-1]
    hidden = narrow.shape[-1]

    def mate(chip, core):
        return lax.rem(rank + 2 * chip - lax.rem(rank, 2), GROUP) + lax.rem(rank + core, 2)

    def remote(src, dst, send, recv, device):
        return pltpu.make_async_remote_copy(
            src_ref=src, dst_ref=dst, send_sem=send, recv_sem=recv,
            device_id={"blk": device}, device_id_type=MESH,
        )

    def weight_copies(layer):
        return (
            pltpu.make_async_copy(proj_hbm.at[layer], proj.at[layer], weight_sem.at[layer, 0]),
            pltpu.make_async_copy(taps_hbm.at[layer], taps.at[layer], weight_sem.at[layer, 1]),
            pltpu.make_async_copy(outp_hbm.at[layer], outp.at[layer], weight_sem.at[layer, 2]),
        )

    def own_in(chunk):
        return pltpu.make_async_copy(
            x_hbm.at[:, rank, chunk], xt.at[chunk, pl.ds(halves * rank, halves)], own_sem.at[chunk]
        )

    for copy in weight_copies(0):
        copy.start()

    @pl.loop(0, chunks)
    def _(chunk):
        own_in(chunk).start()

    barrier = pltpu.get_barrier_semaphore()
    for step in ORDER:
        pl.semaphore_signal(barrier, inc=1, device_id={"blk": base + mate(*step)}, device_id_type=MESH)
    for device in (above, below):
        pl.semaphore_signal(barrier, inc=1, device_id={"blk": device}, device_id_type=MESH)
    pl.semaphore_wait(barrier, GROUP + 1)

    def send_in(chunk):
        for step in ORDER:
            to = mate(*step)
            remote(
                x_hbm.at[:, to, chunk], xt.at[chunk, pl.ds(halves * rank, halves)],
                in_send.at[chunk], in_recv.at[chunk], base + to,
            ).start()

    @pl.loop(0, AHEAD)
    def _(chunk):
        send_in(chunk)

    for layer in range(1, LAYERS):
        for copy in weight_copies(layer):
            copy.start()

    def halo_copies(layer, chunk):
        reach = 2**layer
        mine = narrow.at[chunk, layer]
        up = remote(
            mine.at[pl.ds(span // 2 + span - reach, reach)], mine.at[pl.ds(span // 2 - reach, reach)],
            halo_send.at[chunk, layer, 0], halo_recv.at[chunk, layer, 0], above,
        )
        down = remote(
            mine.at[pl.ds(span // 2, reach)], mine.at[pl.ds(span // 2 + span, reach)],
            halo_send.at[chunk, layer, 1], halo_recv.at[chunk, layer, 1], below,
        )
        return up, down

    def stream_of(chunk):
        return xt[chunk].reshape(rows, width).astype(F32)

    def project(values, layer, chunk):
        centred = values - jnp.mean(values, axis=1, keepdims=True)
        variance = jnp.mean(centred * centred, axis=1, keepdims=True)
        normed = centred * lax.rsqrt(variance + EPSILON) * gain_ref[pl.ds(layer, 1), :] + bias_ref[pl.ds(layer, 1), :]
        result = jnp.dot(normed.astype(BF16), proj[layer], preferred_element_type=F32).astype(BF16)
        narrow[chunk, layer, pl.ds(span // 2, span)] = result.reshape(span, SLAB, hidden)

    def update(layer, chunk):
        reach = jnp.where(layer == 0, 1, jnp.where(layer == 1, 2, jnp.where(layer == 2, 4, 8)))
        parts = [
            narrow[chunk, layer, pl.ds(span // 2 + shift, span)].reshape(rows, hidden)
            for shift in (-reach, 0, reach)
        ]
        convolved = jnp.dot(
            jnp.concatenate(parts, axis=1), taps[layer], preferred_element_type=F32
        )
        activated = gelu(convolved).astype(BF16)
        delta = jnp.dot(activated, outp[layer], preferred_element_type=F32)
        new = (stream_of(chunk) + delta).astype(BF16)
        xt[chunk] = new.reshape(span, SLAB, width)
        return new.astype(F32)

    def own_out(chunk):
        return pltpu.make_async_copy(
            xt.at[chunk, pl.ds(halves * rank, halves)], out_ref.at[:, rank, chunk], out_own.at[chunk]
        )

    def out_copies(chunk):
        return [
            remote(
                xt.at[chunk, pl.ds(halves * mate(*step), halves)], out_ref.at[:, rank, chunk],
                out_send.at[chunk], out_recv.at[chunk], base + mate(*step),
            )
            for step in ORDER
        ]

    def step(stage, chunk):
        @pl.when(stage == 0)
        def _():
            own_in(chunk).wait()
            whole = xt.at[chunk, pl.ds(0, span - halves)]
            pltpu.make_async_copy(whole, whole, in_recv.at[chunk]).wait()

            @pl.when(chunk + AHEAD < chunks)
            def _():
                send_in(chunk + AHEAD)

        for layer in range(LAYERS):
            @pl.when((stage == layer) & (chunk == 0))
            def _():
                for copy in weight_copies(layer):
                    copy.wait()

            @pl.when(stage == layer + 1)
            def _():
                for copy in halo_copies(layer, chunk):
                    copy.wait_recv()

        @pl.when(stage == 0)
        def _():
            project(stream_of(chunk), 0, chunk)

        @pl.when((stage > 0) & (stage < LAYERS))
        def _():
            project(update(stage - 1, chunk), stage, chunk)

        @pl.when(stage == LAYERS)
        def _():
            update(LAYERS - 1, chunk)

        for layer in range(LAYERS):
            @pl.when(stage == layer)
            def _():
                for copy in halo_copies(layer, chunk):
                    copy.start()

        @pl.when(stage == LAYERS)
        def _():
            own_out(chunk).start()
            for copy in out_copies(chunk):
                copy.start()

    order = [divmod(item, 10) for item in SCHEDULE]
    words = [
        sum((stage * 4 + chunk) << 5 * i for i, (stage, chunk) in enumerate(order[at : at + 6]))
        for at in range(0, len(order), 6)
    ]

    def advance(_, codes):
        item = codes[0] & 31
        step(item >> 2, item & 3)
        rest = [(codes[i] >> 5) + ((codes[i + 1] & 31) << 25) for i in range(len(codes) - 1)]
        return (*rest, codes[-1] >> 5)

    lax.fori_loop(0, len(order), advance, tuple(jnp.int32(word) for word in words))

    @pl.loop(0, chunks)
    def _(chunk):
        whole = xt.at[chunk, pl.ds(0, span - halves)]
        own_out(chunk).wait()
        for layer in range(LAYERS):
            for copy in halo_copies(layer, chunk):
                copy.wait_send()
        pltpu.make_async_copy(whole, whole, in_send.at[chunk]).wait()
        pltpu.make_async_copy(whole, whole, out_send.at[chunk]).wait()
        pltpu.make_async_copy(whole, whole, out_recv.at[chunk]).wait()


def solution(mesh):
    peers = mesh.shape["blk"]

    def body(stream, norm_gain, norm_bias, proj_in, convolution_taps, output_projection):
        rows, width = stream.shape
        hidden = proj_in.shape[2]
        halves = rows // UNIT
        chunks = UNIT // GROUP // SLAB
        span = GROUP * halves
        shape = (halves, GROUP, chunks, SLAB, width)
        vmem = pl.BlockSpec(memory_space=pltpu.VMEM)
        anywhere = pl.BlockSpec(memory_space=pl.ANY)
        dma = pltpu.SemaphoreType.DMA
        result = pl.pallas_call(
            functools.partial(kernel, peers, halves, chunks),
            out_shape=pltpu.VMEM(shape, BF16),
            in_specs=[anywhere, vmem, vmem, anywhere, anywhere, anywhere],
            out_specs=vmem,
            scratch_shapes=[
                pltpu.VMEM((chunks, span, SLAB, width), BF16),
                pltpu.VMEM((chunks, LAYERS, 2 * span, SLAB, hidden), BF16),
                pltpu.VMEM((LAYERS, width, hidden), BF16),
                pltpu.VMEM((LAYERS, 3 * hidden, hidden), BF16),
                pltpu.VMEM((LAYERS, hidden, width), BF16),
                dma((chunks,)), dma((chunks,)), dma((chunks,)),
                dma((chunks, LAYERS, 2)), dma((chunks, LAYERS, 2)),
                dma((chunks,)), dma((chunks,)), dma((chunks,)),
                dma((LAYERS, 3)),
            ],
            compiler_params=pltpu.CompilerParams(
                collective_id=0, has_side_effects=True, vmem_limit_bytes=56 * 2**20
            ),
        )(
            stream.reshape(shape), norm_gain, norm_bias, proj_in,
            convolution_taps.reshape(LAYERS, 3 * hidden, hidden), output_projection,
        )
        return result.reshape(rows, width)

    return jax.shard_map(
        body,
        mesh=mesh,
        in_specs=(P(("batch", "blk"), None), P(), P(), P(), P(), P()),
        out_specs=P(("batch", "blk"), None),
        check_vma=False,
    )
```

```python
import functools

import jax
import jax.numpy as jnp
from jax import lax
from jax.experimental import pallas as pl
from jax.experimental.pallas import tpu as pltpu
from jax.sharding import PartitionSpec as P

MESH = pl.DeviceIdType.MESH
LAYERS = 4
UNIT = 512
EPSILON = 1e-05
GROUP = 8
SLAB = 16
BF16 = jnp.bfloat16
F32 = jnp.float32


def gelu(values):
    return 0.5 * values * (1.0 + lax.erf(values * 0.7071067811865476))


def kernel(
    peers, halves, chunks,
    x_hbm, gain_ref, bias_ref, proj_hbm, taps_hbm, outp_hbm,
    out_ref,
    xt, narrow, proj, taps, outp,
    in_send, in_recv, own_sem, halo_send, halo_recv, out_send, out_recv, out_own, weight_sem,
):
    me = lax.axis_index("blk")
    rank = lax.rem(me, GROUP)
    base = me - rank
    above = lax.rem(me + GROUP, peers)
    below = lax.rem(me + peers - GROUP, peers)
    span = GROUP * halves
    rows = span * SLAB
    width = x_hbm.shape[-1]
    hidden = narrow.shape[-1]

    def mate(step):
        return lax.rem(rank + step, GROUP)

    def remote(src, dst, send, recv, device):
        return pltpu.make_async_remote_copy(
            src_ref=src, dst_ref=dst, send_sem=send, recv_sem=recv,
            device_id={"blk": device}, device_id_type=MESH,
        )

    def weight_copies(layer):
        return (
            pltpu.make_async_copy(proj_hbm.at[layer], proj.at[layer], weight_sem.at[layer, 0]),
            pltpu.make_async_copy(taps_hbm.at[layer], taps.at[layer], weight_sem.at[layer, 1]),
            pltpu.make_async_copy(outp_hbm.at[layer], outp.at[layer], weight_sem.at[layer, 2]),
        )

    def own_in(chunk):
        return pltpu.make_async_copy(
            x_hbm.at[:, rank, chunk], xt.at[chunk, pl.ds(halves * rank, halves)], own_sem.at[chunk]
        )

    for copy in weight_copies(0):
        copy.start()

    @pl.loop(0, chunks)
    def _(chunk):
        own_in(chunk).start()

    barrier = pltpu.get_barrier_semaphore()
    for step in range(1, GROUP):
        pl.semaphore_signal(barrier, inc=1, device_id={"blk": base + mate(step)}, device_id_type=MESH)
    for device in (above, below):
        pl.semaphore_signal(barrier, inc=1, device_id={"blk": device}, device_id_type=MESH)
    pl.semaphore_wait(barrier, GROUP + 1)

    @pl.loop(0, chunks)
    def _(chunk):
        for step in (4, 5, 3, 6, 2, 7, 1):
            to = mate(step)
            remote(
                x_hbm.at[:, to, chunk], xt.at[chunk, pl.ds(halves * rank, halves)],
                in_send.at[chunk], in_recv.at[chunk], base + to,
            ).start()

    for layer in range(1, LAYERS):
        for copy in weight_copies(layer):
            copy.start()

    def halo_copies(layer, chunk):
        reach = 2**layer
        mine = narrow.at[chunk, layer]
        up = remote(
            mine.at[pl.ds(span // 2 + span - reach, reach)], mine.at[pl.ds(span // 2 - reach, reach)],
            halo_send.at[chunk, layer, 0], halo_recv.at[chunk, layer, 0], above,
        )
        down = remote(
            mine.at[pl.ds(span // 2, reach)], mine.at[pl.ds(span // 2 + span, reach)],
            halo_send.at[chunk, layer, 1], halo_recv.at[chunk, layer, 1], below,
        )
        return up, down

    def stream_of(chunk):
        return xt[chunk].reshape(rows, width).astype(F32)

    def project(values, layer, chunk):
        centred = values - jnp.mean(values, axis=1, keepdims=True)
        variance = jnp.mean(centred * centred, axis=1, keepdims=True)
        normed = centred * lax.rsqrt(variance + EPSILON) * gain_ref[pl.ds(layer, 1), :] + bias_ref[pl.ds(layer, 1), :]
        result = jnp.dot(normed.astype(BF16), proj[layer], preferred_element_type=F32).astype(BF16)
        narrow[chunk, layer, pl.ds(span // 2, span)] = result.reshape(span, SLAB, hidden)

    def rows_at(layer, chunk, shift):
        return narrow[chunk, layer, pl.ds(span // 2 + shift, span)].reshape(rows, hidden)

    def update(layer, chunk):
        reach = 2**layer
        halos = halo_copies(layer, chunk)
        middle = jnp.dot(rows_at(layer, chunk, 0), taps[layer, pl.ds(hidden, hidden)], preferred_element_type=F32)
        for copy in halos:
            copy.wait_recv()
        before = jnp.dot(rows_at(layer, chunk, -reach), taps[layer, pl.ds(0, hidden)], preferred_element_type=F32)
        after = jnp.dot(rows_at(layer, chunk, reach), taps[layer, pl.ds(2 * hidden, hidden)], preferred_element_type=F32)
        convolved = before + middle + after
        activated = gelu(convolved).astype(BF16)
        delta = jnp.dot(activated, outp[layer], preferred_element_type=F32)
        new = (stream_of(chunk) + delta).astype(BF16)
        xt[chunk] = new.reshape(span, SLAB, width)
        return new.astype(F32)

    def own_out(chunk):
        return pltpu.make_async_copy(
            xt.at[chunk, pl.ds(halves * rank, halves)], out_ref.at[:, rank, chunk], out_own.at[chunk]
        )

    def out_copies(chunk):
        return [
            remote(
                xt.at[chunk, pl.ds(halves * mate(step), halves)], out_ref.at[:, rank, chunk],
                out_send.at[chunk], out_recv.at[chunk], base + mate(step),
            )
            for step in (4, 5, 3, 6, 2, 7, 1)
        ]

    stages = LAYERS + 1

    @pl.loop(0, stages + chunks - 1)
    def _(wave):
        @pl.loop(0, chunks)
        def _(chunk):
            stage = wave - chunk

            @pl.when(stage == 0)
            def _():
                own_in(chunk).wait()
                whole = xt.at[chunk, pl.ds(0, span - halves)]
                pltpu.make_async_copy(whole, whole, in_recv.at[chunk]).wait()

            @pl.when((stage == 0) & (chunk == 0))
            def _():
                for copy in weight_copies(0):
                    copy.wait()

            @pl.when(stage == 0)
            def _():
                project(stream_of(chunk), 0, chunk)
                for copy in halo_copies(0, chunk):
                    copy.start()

            for layer in range(1, LAYERS):
                @pl.when((stage == layer) & (chunk == 0))
                def _():
                    for copy in weight_copies(layer):
                        copy.wait()

            for layer in range(LAYERS):
                @pl.when(stage == layer + 1)
                def _():
                    new = update(layer, chunk)
                    if layer + 1 < LAYERS:
                        project(new, layer + 1, chunk)
                        for copy in halo_copies(layer + 1, chunk):
                            copy.start()

            @pl.when(stage == LAYERS)
            def _():
                own_out(chunk).start()
                for copy in out_copies(chunk):
                    copy.start()

    @pl.loop(0, chunks)
    def _(chunk):
        whole = xt.at[chunk, pl.ds(0, span - halves)]
        own_out(chunk).wait()
        for layer in range(LAYERS):
            for copy in halo_copies(layer, chunk):
                copy.wait_send()
        pltpu.make_async_copy(whole, whole, in_send.at[chunk]).wait()
        pltpu.make_async_copy(whole, whole, out_send.at[chunk]).wait()
        pltpu.make_async_copy(whole, whole, out_recv.at[chunk]).wait()


def solution(mesh):
    peers = mesh.shape["blk"]

    def body(stream, norm_gain, norm_bias, proj_in, convolution_taps, output_projection):
        rows, width = stream.shape
        hidden = proj_in.shape[2]
        halves = rows // UNIT
        chunks = UNIT // GROUP // SLAB
        span = GROUP * halves
        shape = (halves, GROUP, chunks, SLAB, width)
        vmem = pl.BlockSpec(memory_space=pltpu.VMEM)
        anywhere = pl.BlockSpec(memory_space=pl.ANY)
        dma = pltpu.SemaphoreType.DMA
        result = pl.pallas_call(
            functools.partial(kernel, peers, halves, chunks),
            out_shape=pltpu.VMEM(shape, BF16),
            in_specs=[anywhere, vmem, vmem, anywhere, anywhere, anywhere],
            out_specs=vmem,
            scratch_shapes=[
                pltpu.VMEM((chunks, span, SLAB, width), BF16),
                pltpu.VMEM((chunks, LAYERS, 2 * span, SLAB, hidden), BF16),
                pltpu.VMEM((LAYERS, width, hidden), BF16),
                pltpu.VMEM((LAYERS, 3 * hidden, hidden), BF16),
                pltpu.VMEM((LAYERS, hidden, width), BF16),
                dma((chunks,)), dma((chunks,)), dma((chunks,)),
                dma((chunks, LAYERS, 2)), dma((chunks, LAYERS, 2)),
                dma((chunks,)), dma((chunks,)), dma((chunks,)),
                dma((LAYERS, 3)),
            ],
            compiler_params=pltpu.CompilerParams(
                collective_id=0, has_side_effects=True, vmem_limit_bytes=56 * 2**20
            ),
        )(
            stream.reshape(shape), norm_gain, norm_bias, proj_in,
            convolution_taps.reshape(LAYERS, 3 * hidden, hidden), output_projection,
        )
        return result.reshape(rows, width)

    return jax.shard_map(
        body,
        mesh=mesh,
        in_specs=(P(("batch", "blk"), None), P(), P(), P(), P(), P()),
        out_specs=P(("batch", "blk"), None),
        check_vma=False,
    )
```

```python
import functools

import jax
import jax.numpy as jnp
from jax import lax
from jax.experimental import pallas as pl
from jax.experimental.pallas import tpu as pltpu
from jax.sharding import PartitionSpec as P

MESH = pl.DeviceIdType.MESH
LAYERS = 4
UNIT = 512
EPSILON = 1e-05
GROUP = 8
SLAB = 16
BF16 = jnp.bfloat16
F32 = jnp.float32


def gelu(values):
    return 0.5 * values * (1.0 + lax.erf(values * 0.7071067811865476))


def kernel(
    peers, halves, chunks,
    x_hbm, gain_ref, bias_ref, proj_hbm, taps_hbm, outp_hbm,
    out_ref,
    xt, narrow, proj, taps, outp,
    in_send, in_recv, own_sem, halo_send, halo_recv, out_send, out_recv, out_own, weight_sem,
):
    me = lax.axis_index("blk")
    rank = lax.rem(me, GROUP)
    base = me - rank
    above = lax.rem(me + GROUP, peers)
    below = lax.rem(me + peers - GROUP, peers)
    span = GROUP * halves
    rows = span * SLAB
    width = x_hbm.shape[-1]
    hidden = narrow.shape[-1]

    def mate(step):
        return lax.rem(rank + step, GROUP)

    def remote(src, dst, send, recv, device):
        return pltpu.make_async_remote_copy(
            src_ref=src, dst_ref=dst, send_sem=send, recv_sem=recv,
            device_id={"blk": device}, device_id_type=MESH,
        )

    def weight_copies(layer):
        return (
            pltpu.make_async_copy(proj_hbm.at[layer], proj.at[layer], weight_sem.at[layer, 0]),
            pltpu.make_async_copy(taps_hbm.at[layer], taps.at[layer], weight_sem.at[layer, 1]),
            pltpu.make_async_copy(outp_hbm.at[layer], outp.at[layer], weight_sem.at[layer, 2]),
        )

    def own_in(chunk):
        return pltpu.make_async_copy(
            x_hbm.at[:, rank, chunk], xt.at[chunk, pl.ds(halves * rank, halves)], own_sem.at[chunk]
        )

    barrier = pltpu.get_barrier_semaphore()
    for step in range(1, GROUP):
        pl.semaphore_signal(barrier, inc=1, device_id={"blk": base + mate(step)}, device_id_type=MESH)
    for device in (above, below):
        pl.semaphore_signal(barrier, inc=1, device_id={"blk": device}, device_id_type=MESH)

    for copy in weight_copies(0):
        copy.start()

    @pl.loop(0, chunks)
    def _(chunk):
        own_in(chunk).start()

    pl.semaphore_wait(barrier, GROUP + 1)

    @pl.loop(0, chunks)
    def _(chunk):
        for step in (4, 5, 3, 6, 2, 7, 1):
            to = mate(step)
            remote(
                x_hbm.at[:, to, chunk], xt.at[chunk, pl.ds(halves * rank, halves)],
                in_send.at[chunk], in_recv.at[chunk], base + to,
            ).start()

    for layer in range(1, LAYERS):
        for copy in weight_copies(layer):
            copy.start()

    def halo_copies(layer, chunk):
        reach = 2**layer
        mine = narrow.at[chunk, layer]
        up = remote(
            mine.at[pl.ds(span // 2 + span - reach, reach)], mine.at[pl.ds(span // 2 - reach, reach)],
            halo_send.at[chunk, layer, 0], halo_recv.at[chunk, layer, 0], above,
        )
        down = remote(
            mine.at[pl.ds(span // 2, reach)], mine.at[pl.ds(span // 2 + span, reach)],
            halo_send.at[chunk, layer, 1], halo_recv.at[chunk, layer, 1], below,
        )
        return up, down

    def stream_of(chunk):
        return xt[chunk].reshape(rows, width).astype(F32)

    def project(values, layer, chunk):
        centred = values - jnp.mean(values, axis=1, keepdims=True)
        variance = jnp.mean(centred * centred, axis=1, keepdims=True)
        normed = centred * lax.rsqrt(variance + EPSILON) * gain_ref[pl.ds(layer, 1), :] + bias_ref[pl.ds(layer, 1), :]
        result = jnp.dot(normed.astype(BF16), proj[layer], preferred_element_type=F32).astype(BF16)
        narrow[chunk, layer, pl.ds(span // 2, span)] = result.reshape(span, SLAB, hidden)

    def rows_at(layer, chunk, shift):
        return narrow[chunk, layer, pl.ds(span // 2 + shift, span)].reshape(rows, hidden)

    def update(layer, chunk):
        reach = 2**layer
        halos = halo_copies(layer, chunk)
        middle = jnp.dot(rows_at(layer, chunk, 0), taps[layer, pl.ds(hidden, hidden)], preferred_element_type=F32)
        for copy in halos:
            copy.wait_recv()
        before = jnp.dot(rows_at(layer, chunk, -reach), taps[layer, pl.ds(0, hidden)], preferred_element_type=F32)
        after = jnp.dot(rows_at(layer, chunk, reach), taps[layer, pl.ds(2 * hidden, hidden)], preferred_element_type=F32)
        convolved = before + middle + after
        activated = gelu(convolved).astype(BF16)
        delta = jnp.dot(activated, outp[layer], preferred_element_type=F32)
        new = (stream_of(chunk) + delta).astype(BF16)
        xt[chunk] = new.reshape(span, SLAB, width)
        return new.astype(F32)

    def own_out(chunk):
        return pltpu.make_async_copy(
            xt.at[chunk, pl.ds(halves * rank, halves)], out_ref.at[:, rank, chunk], out_own.at[chunk]
        )

    def out_copies(chunk):
        return [
            remote(
                xt.at[chunk, pl.ds(halves * mate(step), halves)], out_ref.at[:, rank, chunk],
                out_send.at[chunk], out_recv.at[chunk], base + mate(step),
            )
            for step in (4, 5, 3, 6, 2, 7, 1)
        ]

    stages = LAYERS + 1

    @pl.loop(0, stages + chunks - 1)
    def _(wave):
        @pl.loop(0, chunks)
        def _(chunk):
            stage = wave - chunk

            @pl.when(stage == 0)
            def _():
                own_in(chunk).wait()
                whole = xt.at[chunk, pl.ds(0, span - halves)]
                pltpu.make_async_copy(whole, whole, in_recv.at[chunk]).wait()

            @pl.when((stage == 0) & (chunk == 0))
            def _():
                for copy in weight_copies(0):
                    copy.wait()

            @pl.when(stage == 0)
            def _():
                project(stream_of(chunk), 0, chunk)
                for copy in halo_copies(0, chunk):
                    copy.start()

            for layer in range(1, LAYERS):
                @pl.when((stage == layer) & (chunk == 0))
                def _():
                    for copy in weight_copies(layer):
                        copy.wait()

            for layer in range(LAYERS):
                @pl.when(stage == layer + 1)
                def _():
                    new = update(layer, chunk)
                    if layer + 1 < LAYERS:
                        project(new, layer + 1, chunk)
                        for copy in halo_copies(layer + 1, chunk):
                            copy.start()

            @pl.when(stage == LAYERS)
            def _():
                own_out(chunk).start()
                for copy in out_copies(chunk):
                    copy.start()

    @pl.loop(0, chunks)
    def _(chunk):
        whole = xt.at[chunk, pl.ds(0, span - halves)]
        own_out(chunk).wait()
        for layer in range(LAYERS):
            for copy in halo_copies(layer, chunk):
                copy.wait_send()
        pltpu.make_async_copy(whole, whole, in_send.at[chunk]).wait()
        pltpu.make_async_copy(whole, whole, out_send.at[chunk]).wait()
        pltpu.make_async_copy(whole, whole, out_recv.at[chunk]).wait()


def solution(mesh):
    peers = mesh.shape["blk"]

    def body(stream, norm_gain, norm_bias, proj_in, convolution_taps, output_projection):
        rows, width = stream.shape
        hidden = proj_in.shape[2]
        halves = rows // UNIT
        chunks = UNIT // GROUP // SLAB
        span = GROUP * halves
        shape = (halves, GROUP, chunks, SLAB, width)
        vmem = pl.BlockSpec(memory_space=pltpu.VMEM)
        anywhere = pl.BlockSpec(memory_space=pl.ANY)
        dma = pltpu.SemaphoreType.DMA
        result = pl.pallas_call(
            functools.partial(kernel, peers, halves, chunks),
            out_shape=pltpu.VMEM(shape, BF16),
            in_specs=[anywhere, vmem, vmem, anywhere, anywhere, anywhere],
            out_specs=vmem,
            scratch_shapes=[
                pltpu.VMEM((chunks, span, SLAB, width), BF16),
                pltpu.VMEM((chunks, LAYERS, 2 * span, SLAB, hidden), BF16),
                pltpu.VMEM((LAYERS, width, hidden), BF16),
                pltpu.VMEM((LAYERS, 3 * hidden, hidden), BF16),
                pltpu.VMEM((LAYERS, hidden, width), BF16),
                dma((chunks,)), dma((chunks,)), dma((chunks,)),
                dma((chunks, LAYERS, 2)), dma((chunks, LAYERS, 2)),
                dma((chunks,)), dma((chunks,)), dma((chunks,)),
                dma((LAYERS, 3)),
            ],
            compiler_params=pltpu.CompilerParams(
                collective_id=0, has_side_effects=True, vmem_limit_bytes=56 * 2**20
            ),
        )(
            stream.reshape(shape), norm_gain, norm_bias, proj_in,
            convolution_taps.reshape(LAYERS, 3 * hidden, hidden), output_projection,
        )
        return result.reshape(rows, width)

    return jax.shard_map(
        body,
        mesh=mesh,
        in_specs=(P(("batch", "blk"), None), P(), P(), P(), P(), P()),
        out_specs=P(("batch", "blk"), None),
        check_vma=False,
    )
```
